512 devices in a mesh: img: 32 (over x, z_hi, core), py: 4 (over y), px: 4 (over z_lo).
Axes of the slice: x: 4, y: 4, z: 16 (z_hi: 4, z_lo: 4; z = z_hi * 4 + z_lo), core: 2. Of those that a mesh axis runs over, the one named last changes fastest.
Arguments:
- queries: bfloat16 [32, 64, 64, 1536], P('img', 'py', 'px')
- keys: bfloat16 [32, 64, 64, 1536], P('img', 'py', 'px')
- values: bfloat16 [32, 64, 64, 1536], P('img', 'py', 'px'), may hold values from -6 to 6
- pattern: int32 [32, 8, 8, 9], P('img', 'py', 'px'), may hold values from 0 to 1, as said below
- targets: int32 [32, 8, 8, 12, 3], P('img', 'py', 'px'), may hold values from 0 to 8, as said below
- router_q: float32 [12, 128, 64], replicated, may hold values from -1.5 to 1.5
- router_k: float32 [12, 128, 64], replicated, may hold values from -1.5 to 1.5
Outputs:
- attended: bfloat16 [32, 64, 64, 1536], P('img', 'py', 'px')
- grad_q: float32 [12, 128, 64], replicated
- grad_k: float32 [12, 128, 64], replicated
The draws below stay inside these ranges and needn't reach their ends.
Inputs may be any that keep to these rules, and one draw needn't show every extreme that they name: `pattern`: the centre offset and the offsets one block away along one axis that lie in the image are 1; offsets outside the image are 0. `targets`: 3 different offsets per query block and head, each with pattern 1.
All inputs are finite; a program needn't handle non-finite values.
Results may differ from the reference program's by a relative error of at most 0.0049.
Values may be sent and summed in bfloat16 or wider, within the bound.
No kernel may reach another device: no remote copies, remote signals or barrier semaphores. Data moves between devices by JAX's collectives and lax.ppermute only.
A program may use at most 64 MiB of HBM per device.

```python
import math
import jax
import jax.numpy as jnp
from jax import lax

HEADS = 12
DH = 128
RW = 64
BS = 8
RADIUS = 1
TOPK = 3
NOFF = 9
FEAT = 1536
IMAGES = 32
NBY = 8
NBX = 8
NY = 64
NX = 64


def draw_field(key, salt):
    base_key = jax.random.fold_in(key, salt)
    shape = (IMAGES, NY, NX, FEAT)
    base = jax.random.normal(base_key, shape, jnp.float32)
    base = jnp.clip(base, -6.0, 6.0)
    return base.astype(jnp.bfloat16)


def draw_queries(key, part):
    return draw_field(key, 11)


def draw_keys(key, part):
    return draw_field(key, 12)


def block_layout(key):
    width = 2 * RADIUS + 1
    rows = jnp.arange(NBY, dtype=jnp.int32)[:, None, None]
    cols = jnp.arange(NBX, dtype=jnp.int32)[None, :, None]
    offs = jnp.arange(NOFF, dtype=jnp.int32)
    shift_y = offs // width - RADIUS
    shift_x = offs % width - RADIUS
    inside = (rows + shift_y >= 0) & (rows + shift_y < NBY) & (cols + shift_x >= 0) & (cols + shift_x < NBX)
    core = jnp.abs(shift_y) + jnp.abs(shift_x) <= 1
    coin = jax.random.randint(jax.random.fold_in(key, 201), (IMAGES, NBY, NBX, NOFF), 0, 8)
    live = inside[None] & (core[None, None, None, :] | (coin < 5))
    return live.astype(jnp.int32)


def draw_pattern(key, part):
    return block_layout(key)


def draw_targets(key, part):
    live = block_layout(key)
    noise = jax.random.randint(jax.random.fold_in(key, 202), (IMAGES, NBY, NBX, HEADS, NOFF), 0, 2 ** 20)
    offs = jnp.arange(NOFF, dtype=jnp.int32)
    score = noise * 32 + offs + live[:, :, :, None, :] * 2 ** 26
    return lax_top(score)


def lax_top(score):
    return jax.lax.top_k(score, TOPK)[1].astype(jnp.int32)


def levels(key, shape, cuts, least, top_value):
    def one(axis_at, parts):
        heights = jax.random.uniform(jax.random.fold_in(jax.random.fold_in(key, 6), axis_at), (parts,), jnp.float32, least / len(cuts), top_value / len(cuts))
        return jnp.repeat(jnp.exp(heights), shape[axis_at] // parts).reshape((-1,) + (1,) * (len(shape) - axis_at - 1))

    loudness = one(*cuts[0])
    for cut in cuts[1:]:
        loudness = loudness * one(*cut)
    return loudness


def scatter_about(own_key, extent, spread, bound, shards=(), held_as=jnp.bfloat16):
    values = jax.random.normal(own_key, extent, jnp.float32) * spread
    if len(shards) > 0:
        values = levels(own_key, extent, shards, -0.22, 0.18) * values
    return jnp.clip(values, min=-bound, max=bound).astype(held_as)


def setup_inputs(seed: int = 0) -> dict:
    key_of = jax.random.split(jax.random.key(seed), 8)
    queries = draw_queries(jax.random.fold_in(key_of[7], 71), 0)
    keys = draw_keys(jax.random.fold_in(key_of[7], 71), 0)
    values = scatter_about(key_of[2], (IMAGES, NY, NX, FEAT), 1.0, 6.0, ((0, 32), (1, 4), (2, 4)))
    pattern = draw_pattern(jax.random.fold_in(key_of[7], 71), 0)
    targets = draw_targets(jax.random.fold_in(key_of[7], 71), 0)
    router_q = scatter_about(key_of[5], (HEADS, DH, RW), (DH // 8) ** -0.5, 1.5, (), jnp.float32)
    router_k = scatter_about(key_of[6], (HEADS, DH, RW), (DH // 8) ** -0.5, 1.5, (), jnp.float32)
    return dict(queries=queries, keys=keys, values=values, pattern=pattern, targets=targets, router_q=router_q, router_k=router_k)


def attend(query_tile, key_ext, value_ext, live):
    tile_y, tile_x, feat = query_tile.shape
    blocks_y = tile_y // BS
    blocks_x = tile_x // BS
    width = 2 * RADIUS + 1
    side = width * BS
    scale = 1.0 / math.sqrt(DH)
    anchor = jnp.zeros((), jnp.int32)

    def regroup(window):
        return window.reshape(width, BS, width, BS, feat).transpose(0, 2, 1, 3, 4).reshape(NOFF * BS * BS, HEADS, DH)

    def one_block(index):
        row = (index // blocks_x).astype(jnp.int32)
        col = (index % blocks_x).astype(jnp.int32)
        start_y = (row * BS).astype(jnp.int32)
        start_x = (col * BS).astype(jnp.int32)
        query = lax.dynamic_slice(query_tile, (start_y, start_x, anchor), (BS, BS, feat)).reshape(BS * BS, HEADS, DH)
        window_k = regroup(lax.dynamic_slice(key_ext, (start_y, start_x, anchor), (side, side, feat)))
        window_v = regroup(lax.dynamic_slice(value_ext, (start_y, start_x, anchor), (side, side, feat)))
        mask_row = lax.dynamic_slice(live, (row, col, anchor), (1, 1, NOFF)).reshape(NOFF)
        key_mask = jnp.repeat(mask_row, BS * BS) > 0
        scores = jnp.einsum('qhd,khd->hqk', query, window_k, preferred_element_type=jnp.float32) * scale
        scores = jnp.where(key_mask[None, None, :], scores, -1e+30)
        top = lax.optimization_barrier(jnp.max(scores, axis=-1, keepdims=True))
        weights = jnp.exp(scores - top)
        probs = (weights / lax.optimization_barrier(jnp.sum(weights, axis=-1, keepdims=True))).astype(jnp.bfloat16)
        out = jnp.einsum('hqk,khd->qhd', probs, window_v, preferred_element_type=jnp.float32)
        return out.astype(jnp.bfloat16).reshape(BS, BS, feat)
    outs = lax.map(one_block, jnp.arange(blocks_y * blocks_x, dtype=jnp.int32))
    return outs.reshape(blocks_y, blocks_x, BS, BS, feat).transpose(0, 2, 1, 3, 4).reshape(tile_y, tile_x, feat)

def pooling(tile):
    tile_y, tile_x, feat = tile.shape
    shaped = tile.reshape(tile_y // BS, BS, tile_x // BS, BS, HEADS, DH)
    return lax.optimization_barrier(jnp.sum(shaped, axis=(1, 3), dtype=jnp.float32)) / (BS * BS)

def router_loss(weights_q, weights_k, pooled_q, pooled_k, live, chosen):
    route_q = jnp.einsum('yxhd,hdr->yxhr', pooled_q, weights_q, precision=lax.Precision.HIGHEST)
    route_k = jnp.einsum('yxhd,hdr->yxhr', pooled_k, weights_k, precision=lax.Precision.HIGHEST)
    blocks_y, blocks_x = (pooled_q.shape[0], pooled_q.shape[1])
    width = 2 * RADIUS + 1
    shifted = jnp.stack([route_k[up:up + blocks_y, left:left + blocks_x] for up in range(width) for left in range(width)], axis=2)
    logits = jnp.einsum('yxhr,yxohr->yxho', route_q, shifted, precision=lax.Precision.HIGHEST) / math.sqrt(RW)
    logits = jnp.where(live[:, :, None, :] > 0, logits, -1e+30)
    top = lax.optimization_barrier(jnp.max(logits, axis=-1, keepdims=True))
    logz = top + jnp.log(lax.optimization_barrier(jnp.sum(jnp.exp(logits - top), axis=-1, keepdims=True)))
    logp = logits - logz
    picks = (chosen[..., None] == jnp.arange(NOFF, dtype=jnp.int32)).astype(jnp.float32)
    return -jnp.sum(picks * logp[:, :, :, None, :])

def reference(queries, keys, values, pattern, targets, router_q, router_k):
    rim = RADIUS * BS

    def image_out(items):
        query_img, key_img, value_img, live = items
        key_pad = jnp.pad(key_img, ((rim, rim), (rim, rim), (0, 0)))
        value_pad = jnp.pad(value_img, ((rim, rim), (rim, rim), (0, 0)))
        return attend(query_img, key_pad, value_pad, live)
    attended = lax.map(image_out, (queries, keys, values, pattern))
    pooled_q = lax.map(pooling, queries)
    pooled_k = lax.map(pooling, keys)
    pooled_k = jnp.pad(pooled_k, ((0, 0), (RADIUS, RADIUS), (RADIUS, RADIUS), (0, 0), (0, 0)))
    normal = float(TOPK * HEADS * NBY * NBX)

    def total_loss(weights_q, weights_k):

        def one_image(items):
            pq, pk, live, chosen = items
            return router_loss(weights_q, weights_k, pq, pk, live, chosen)
        return jnp.sum(lax.map(one_image, (pooled_q, pooled_k, pattern, targets))) / normal
    grad_q, grad_k = jax.grad(total_loss, argnums=(0, 1))(router_q, router_k)
    return (attended, grad_q, grad_k)
```

```python
import functools
import math

import jax
import jax.numpy as jnp
import numpy as np
from jax import lax
from jax.experimental import pallas as pl
from jax.experimental.pallas import tpu as pltpu
from jax.sharding import PartitionSpec as P

HEADS = 12
DH = 128
RW = 64
BS = 8
TOPK = 3
NOFF = 9
TILE = 16
TOK = TILE * TILE
FEAT = HEADS * DH
EDGE = BS * TILE
NKEY = TOK + 6 * EDGE
SLOTS = 16
HSTEP = 2
LIVE_CAP = 3.4e38
DEAD_CAP = -1e30
TILES = ("py", "px")


def key_block_ids():
    ids = np.zeros((8, NKEY), np.int32)
    own = np.arange(TOK)
    row = [(1 + own // TILE // BS) * 4 + 1 + own % TILE // BS]
    edge = np.arange(EDGE)
    row.append(1 + edge % TILE // BS)
    row.append(12 + 1 + edge % TILE // BS)
    row.append((1 + edge // BS // BS) * 4)
    row.append((1 + edge // BS // BS) * 4 + 3)
    row.append(edge // (BS * BS) * 12)
    row.append(edge // (BS * BS) * 12 + 3)
    ids[:] = np.concatenate(row)[None]
    return ids


def pool_kernel(q_ref, k_ref, aux_ref, out_ref):
    row = lax.broadcasted_iota(jnp.int32, (8, TOK), 0)
    tok = lax.broadcasted_iota(jnp.int32, (8, TOK), 1)
    block = tok // TILE // BS * 2 + tok % TILE // BS
    pick_q = (row == block).astype(jnp.float32).astype(jnp.bfloat16)
    pick_k = (row == block + 4).astype(jnp.float32).astype(jnp.bfloat16)
    sums = jnp.dot(pick_q, q_ref[...], preferred_element_type=jnp.float32)
    sums += jnp.dot(pick_k, k_ref[...], preferred_element_type=jnp.float32)
    means = sums / (BS * BS)
    for h in range(HEADS):
        out_ref[h, 0:8, :] = means[:, h * DH : (h + 1) * DH]
        out_ref[h, 8:16, :] = aux_ref[h]
    for h in range(HEADS, SLOTS):
        out_ref[h] = jnp.zeros((16, DH), jnp.float32)


def pool(query, key, aux):
    return pl.pallas_call(
        pool_kernel,
        out_shape=jax.ShapeDtypeStruct((SLOTS, 16, DH), jnp.float32),
        name="pool",
    )(query, key, aux)


def router_kernel(normal, head_ref, recv_ref, wq_ref, wk_ref, out_ref, pq_ref, pk_ref, ax_ref):
    for i in range(SLOTS):
        pq_ref[4 * i : 4 * i + 4, :] = recv_ref[i, 0:4, :]
        pk_ref[4 * i : 4 * i + 4, :] = recv_ref[i, 4:8, :]
        ax_ref[4 * i : 4 * i + 4, :] = recv_ref[i, 8:12, :]
    n = 4 * SLOTS
    dot = functools.partial(
        lax.dot_general, precision=lax.Precision.HIGHEST, preferred_element_type=jnp.float32
    )
    ab, abt, atb = (((1,), (0,)), ((), ())), (((1,), (1,)), ((), ())), (((0,), (0,)), ((), ()))
    pooled_q, pooled_k, aux = pq_ref[...], pk_ref[...], ax_ref[...]
    route_q = dot(pooled_q, wq_ref[0], ab)
    route_k = dot(pooled_k, wk_ref[0], ab)
    logits = dot(route_q, route_k, abt) / math.sqrt(RW)

    def place(i):
        tile, sub = i // 4, i % 4
        return tile // 4 * 2 + sub // 2, tile % 4 * 2 + sub % 2

    qy, qx = place(lax.broadcasted_iota(jnp.int32, (n, n), 0))
    ky, kx = place(lax.broadcasted_iota(jnp.int32, (n, n), 1))
    up, left = ky - qy + 1, kx - qx + 1
    near = (up >= 0) & (up <= 2) & (left >= 0) & (left <= 2)
    off = jnp.where(near, 3 * up + left, -1).astype(jnp.float32)
    live = jnp.zeros((n, n), jnp.float32)
    for o in range(NOFF):
        live = jnp.where(off == float(o), aux[:, o : o + 1], live)
    picks = jnp.zeros((n, n), jnp.float32)
    for k in range(TOPK):
        picks += (off == aux[:, NOFF + k : NOFF + k + 1]).astype(jnp.float32)
    logits = jnp.where(live > 0.5, logits, -1e30)
    top = jnp.max(logits, axis=1, keepdims=True)
    weights = jnp.exp(logits - top)
    soft = weights / jnp.sum(weights, axis=1, keepdims=True)
    count = jnp.sum(picks, axis=1, keepdims=True)
    slope = jnp.where(live > 0.5, count * soft - picks, 0.0) * (1.0 / (normal * math.sqrt(RW)))
    grad_q = dot(pooled_q, dot(slope, route_k, ab), atb)
    grad_k = dot(pooled_k, dot(slope, route_q, atb), atb)
    out_ref[...] = jnp.concatenate([grad_q, grad_k], axis=1)


def router_grads(head, recv, weights_q, weights_k, normal):
    spec = pl.BlockSpec((1, DH, RW), lambda i, h: (h[0], 0, 0))
    return pl.pallas_call(
        functools.partial(router_kernel, normal),
        out_shape=jax.ShapeDtypeStruct((DH, 2 * RW), jnp.float32),
        grid_spec=pltpu.PrefetchScalarGridSpec(
            num_scalar_prefetch=1,
            grid=(1,),
            in_specs=[
                pl.BlockSpec((SLOTS, 16, DH), lambda i, h: (0, 0, 0)),
                spec,
                spec,
            ],
            out_specs=pl.BlockSpec((DH, 2 * RW), lambda i, h: (0, 0)),
            scratch_shapes=[pltpu.VMEM((4 * SLOTS, DH), jnp.float32)] * 3,
        ),
        name="router",
    )(head, recv, weights_q, weights_k)


def attend_kernel(pat_ref, ids_ref, q_ref, k_ref, v_ref, *rest):
    sides, out_ref, cap_ref = rest[:6], rest[6], rest[7]

    @pl.when(pl.program_id(0) == 0)
    def _():
        ids = ids_ref[...]
        tok = lax.broadcasted_iota(jnp.int32, (TOK, NKEY), 0)
        block = tok // TILE // BS * 2 + tok % TILE // BS
        cap = jnp.full((TOK, NKEY), DEAD_CAP, jnp.float32)
        for b in range(4):
            line = jnp.full((8, NKEY), DEAD_CAP, jnp.float32)
            for o in range(NOFF):
                at = (b // 2 + o // 3) * 4 + b % 2 + o % 3
                value = jnp.where(pat_ref[b, o] > 0, LIVE_CAP, DEAD_CAP)
                line = jnp.where(ids == at, value, line)
            cap = jnp.where(block == b, line[0:1, :], cap)
        cap_ref[...] = cap

    for h in range(HSTEP):
        lanes = slice(h * DH, (h + 1) * DH)
        query = q_ref[:, lanes]
        keys = jnp.concatenate([k_ref[:, lanes]] + [s[0, :, lanes] for s in sides], axis=0)
        values = jnp.concatenate([v_ref[:, lanes]] + [s[1, :, lanes] for s in sides], axis=0)
        scores = lax.dot_general(
            query, keys, (((1,), (1,)), ((), ())), preferred_element_type=jnp.float32
        )
        scores = jnp.minimum(scores, cap_ref[...])
        top = jnp.max(scores, axis=1, keepdims=True)
        weights = jnp.exp2((scores - top) * (math.log2(math.e) / math.sqrt(DH)))
        total = jnp.sum(weights, axis=1, keepdims=True)
        probs = (weights * (1.0 / total)).astype(jnp.bfloat16)
        out = jnp.dot(probs, values, preferred_element_type=jnp.float32)
        out_ref[:, lanes] = out.astype(jnp.bfloat16)


def attend(pattern, query, key, value, sides):
    wide = HSTEP * DH
    own = pl.BlockSpec((TOK, wide), lambda h: (0, h))
    side = pl.BlockSpec((2, EDGE, wide), lambda h: (0, 0, h))
    return pl.pallas_call(
        attend_kernel,
        out_shape=jax.ShapeDtypeStruct((TOK, FEAT), jnp.bfloat16),
        grid=(HEADS // HSTEP,),
        in_specs=[
            pl.BlockSpec(memory_space=pltpu.SMEM),
            pl.BlockSpec((8, NKEY), lambda h: (0, 0)),
            own,
            own,
            own,
        ]
        + [side] * 6,
        out_specs=own,
        scratch_shapes=[pltpu.VMEM((TOK, NKEY), jnp.float32)],
        cost_estimate=pl.CostEstimate(
            flops=4 * HEADS * TOK * NKEY * DH,
            bytes_accessed=2 * FEAT * (2 * TOK + 2 * NKEY),
            transcendentals=HEADS * TOK * NKEY,
        ),
        name="attend",
    )(pattern, jnp.asarray(key_block_ids()), query, key, value, *sides)


def shift(x, axis, step):
    count = lax.axis_size(axis)
    if step > 0:
        pairs = [(i, i + 1) for i in range(count - 1)]
    else:
        pairs = [(i + 1, i) for i in range(count - 1)]
    return lax.ppermute(x, axis, pairs)


def halos(key, value):
    both = (key, value)

    def flat(cut):
        return jnp.stack([cut(x).reshape(EDGE, FEAT) for x in both])

    above = shift(flat(lambda x: x[TILE - BS :]), "py", 1)
    below = shift(flat(lambda x: x[:BS]), "py", -1)
    left = shift(flat(lambda x: x[:, TILE - BS :]), "px", 1)
    right = shift(flat(lambda x: x[:, :BS]), "px", -1)

    def corners(lo):
        cuts = [
            x.reshape(2, BS, TILE, FEAT)[:, :, lo : lo + BS].reshape(2, BS * BS, FEAT)
            for x in (above, below)
        ]
        return jnp.concatenate(cuts, axis=1)

    corner_l = shift(corners(TILE - BS), "px", 1)
    corner_r = shift(corners(0), "px", -1)
    return above, below, left, right, corner_l, corner_r


def everyone(x, axis, count):
    return lax.all_to_all(jnp.broadcast_to(x[None], (count,) + x.shape), axis, 0, 0)


def per_device(queries, keys, values, pattern, targets, router_q, router_k):
    images = lax.axis_size("img")
    tiles_y, tiles_x = lax.axis_size("py"), lax.axis_size("px")
    tiles = tiles_y * tiles_x
    normal = float(TOPK * HEADS * 4 * tiles)
    query, key, value = (x[0].reshape(TOK, FEAT) for x in (queries, keys, values))
    pat = pattern.reshape(4, NOFF)
    aim = targets.reshape(4, HEADS, TOPK).transpose(1, 0, 2)
    aux = jnp.concatenate([jnp.broadcast_to(pat, (HEADS, 4, NOFF)), aim], axis=2)
    aux = jnp.pad(aux.astype(jnp.float32), ((0, 0), (0, 4), (0, DH - NOFF - TOPK)))

    sent = pool(query, key, aux)
    recv = lax.all_to_all(sent, TILES, 0, 0)
    sides = halos(keys[0], values[0])
    me = lax.axis_index("py") * tiles_x + lax.axis_index("px")
    head = jnp.minimum(me, HEADS - 1).astype(jnp.int32).reshape(1)
    grads = router_grads(head, recv, router_q, router_k, normal)
    parts = lax.all_to_all(grads.reshape(images, DH // images, 2 * RW), "img", 0, 0)
    part = jnp.sum(parts, axis=0).astype(jnp.bfloat16)
    mine = everyone(part, "img", images).reshape(DH, 2 * RW)
    every = everyone(mine, TILES, tiles)[:HEADS].astype(jnp.float32)
    attended = attend(pat, query, key, value, sides)
    return (attended.reshape(1, TILE, TILE, FEAT), every[:, :, :RW], every[:, :, RW:])


def solution(mesh):
    return jax.shard_map(
        per_device,
        mesh=mesh,
        in_specs=(
            P("img", "py", "px", None),
            P("img", "py", "px", None),
            P("img", "py", "px", None),
            P("img", "py", "px", None),
            P("img", "py", "px", None, None),
            P(),
            P(),
        ),
        out_specs=(P("img", "py", "px", None), P(), P()),
        check_vma=False,
    )
```

```python
import functools
import math

import jax
import jax.numpy as jnp
import numpy as np
from jax import lax
from jax.experimental import pallas as pl
from jax.experimental.pallas import tpu as pltpu
from jax.sharding import Mesh
from jax.sharding import PartitionSpec as P

HEADS = 12
DH = 128
RW = 64
BS = 8
TOPK = 3
NOFF = 9
TILE = 16
TOK = TILE * TILE
FEAT = HEADS * DH
EDGE = BS * TILE
NKEY = TOK + 6 * EDGE
SLOTS = 16
HSTEP = 2
LIVE_CAP = 3.4e38
DEAD_CAP = -1e30
TILES = ("py", "px")
NEAR = ("x", "core")
IMG = ("x", "far", "core")
IMG_SIZES = (4, 4, 2)


def key_block_ids():
    ids = np.zeros((8, NKEY), np.int32)
    own = np.arange(TOK)
    row = [(1 + own // TILE // BS) * 4 + 1 + own % TILE // BS]
    edge = np.arange(EDGE)
    row.append(1 + edge % TILE // BS)
    row.append(12 + 1 + edge % TILE // BS)
    row.append((1 + edge // BS // BS) * 4)
    row.append((1 + edge // BS // BS) * 4 + 3)
    row.append(edge // (BS * BS) * 12)
    row.append(edge // (BS * BS) * 12 + 3)
    ids[:] = np.concatenate(row)[None]
    return ids


def pool_kernel(q_ref, k_ref, aux_ref, out_ref):
    row = lax.broadcasted_iota(jnp.int32, (8, TOK), 0)
    tok = lax.broadcasted_iota(jnp.int32, (8, TOK), 1)
    block = tok // TILE // BS * 2 + tok % TILE // BS
    pick_q = (row == block).astype(jnp.float32).astype(jnp.bfloat16)
    pick_k = (row == block + 4).astype(jnp.float32).astype(jnp.bfloat16)
    sums = jnp.dot(pick_q, q_ref[...], preferred_element_type=jnp.float32)
    sums += jnp.dot(pick_k, k_ref[...], preferred_element_type=jnp.float32)
    means = sums / (BS * BS)
    for h in range(HEADS):
        out_ref[h, 0:8, :] = means[:, h * DH : (h + 1) * DH]
        out_ref[h, 8:16, :] = aux_ref[h]
    for h in range(HEADS, SLOTS):
        out_ref[h] = jnp.zeros((16, DH), jnp.float32)


def pool(query, key, aux):
    return pl.pallas_call(
        pool_kernel,
        out_shape=jax.ShapeDtypeStruct((SLOTS, 16, DH), jnp.float32),
        name="pool",
    )(query, key, aux)


def router_kernel(normal, head_ref, recv_ref, wq_ref, wk_ref, out_ref, pq_ref, pk_ref, ax_ref):
    for i in range(SLOTS):
        pq_ref[4 * i : 4 * i + 4, :] = recv_ref[i, 0:4, :]
        pk_ref[4 * i : 4 * i + 4, :] = recv_ref[i, 4:8, :]
        ax_ref[4 * i : 4 * i + 4, :] = recv_ref[i, 8:12, :]
    n = 4 * SLOTS
    dot = functools.partial(
        lax.dot_general, precision=lax.Precision.HIGHEST, preferred_element_type=jnp.float32
    )
    ab, abt, atb = (((1,), (0,)), ((), ())), (((1,), (1,)), ((), ())), (((0,), (0,)), ((), ()))
    pooled_q, pooled_k, aux = pq_ref[...], pk_ref[...], ax_ref[...]
    route_q = dot(pooled_q, wq_ref[0], abt)
    route_k = dot(pooled_k, wk_ref[0], abt)
    logits = dot(route_q, route_k, abt) / math.sqrt(RW)

    def place(i):
        tile, sub = i // 4, i % 4
        return tile // 4 * 2 + sub // 2, tile % 4 * 2 + sub % 2

    qy, qx = place(lax.broadcasted_iota(jnp.int32, (n, n), 0))
    ky, kx = place(lax.broadcasted_iota(jnp.int32, (n, n), 1))
    up, left = ky - qy + 1, kx - qx + 1
    near = (up >= 0) & (up <= 2) & (left >= 0) & (left <= 2)
    off = jnp.where(near, 3 * up + left, -1).astype(jnp.float32)
    live = jnp.zeros((n, n), jnp.float32)
    for o in range(NOFF):
        live = jnp.where(off == float(o), aux[:, o : o + 1], live)
    picks = jnp.zeros((n, n), jnp.float32)
    for k in range(TOPK):
        picks += (off == aux[:, NOFF + k : NOFF + k + 1]).astype(jnp.float32)
    logits = jnp.where(live > 0.5, logits, -1e30)
    top = jnp.max(logits, axis=1, keepdims=True)
    weights = jnp.exp(logits - top)
    soft = weights / jnp.sum(weights, axis=1, keepdims=True)
    count = jnp.sum(picks, axis=1, keepdims=True)
    slope = jnp.where(live > 0.5, count * soft - picks, 0.0) * (1.0 / (normal * math.sqrt(RW)))
    out_ref[0:RW, :] = dot(dot(slope, route_k, ab), pooled_q, atb)
    out_ref[RW:, :] = dot(dot(slope, route_q, atb), pooled_k, atb)


def router_grads(head, recv, weights_q, weights_k, normal):
    spec = pl.BlockSpec((1, RW, DH), lambda i, h: (h[0], 0, 0))
    return pl.pallas_call(
        functools.partial(router_kernel, normal),
        out_shape=jax.ShapeDtypeStruct((2 * RW, DH), jnp.float32),
        grid_spec=pltpu.PrefetchScalarGridSpec(
            num_scalar_prefetch=1,
            grid=(1,),
            in_specs=[
                pl.BlockSpec((SLOTS, 16, DH), lambda i, h: (0, 0, 0)),
                spec,
                spec,
            ],
            out_specs=pl.BlockSpec((2 * RW, DH), lambda i, h: (0, 0)),
            scratch_shapes=[pltpu.VMEM((4 * SLOTS, DH), jnp.float32)] * 3,
        ),
        name="router",
    )(head, recv, weights_q, weights_k)


def attend_kernel(pat_ref, ids_ref, q_ref, k_ref, v_ref, *rest):
    sides, (corner_l, corner_r, corner_a, corner_b, out_ref, cap_ref) = rest[:4], rest[4:]
    cell = BS * BS

    @pl.when(pl.program_id(0) == 0)
    def _():
        ids = ids_ref[...]
        tok = lax.broadcasted_iota(jnp.int32, (TOK, NKEY), 0)
        block = tok // TILE // BS * 2 + tok % TILE // BS
        cap = jnp.full((TOK, NKEY), DEAD_CAP, jnp.float32)
        for b in range(4):
            line = jnp.full((8, NKEY), DEAD_CAP, jnp.float32)
            for o in range(NOFF):
                at = (b // 2 + o // 3) * 4 + b % 2 + o % 3
                value = jnp.where(pat_ref[b, o] > 0, LIVE_CAP, DEAD_CAP)
                line = jnp.where(ids == at, value, line)
            cap = jnp.where(block == b, line[0:1, :], cap)
        cap_ref[...] = cap

    for h in range(HSTEP):
        lanes = slice(h * DH, (h + 1) * DH)
        query = q_ref[:, lanes]
        keys = jnp.concatenate(
            [k_ref[:, lanes]]
            + [s[0, :, lanes] for s in sides]
            + [corner_l[:, lanes], corner_r[:, lanes]],
            axis=0,
        )
        values = jnp.concatenate(
            [v_ref[:, lanes]]
            + [s[1, :, lanes] for s in sides]
            + [
                corner_a[:cell, lanes],
                corner_b[:cell, lanes],
                corner_a[cell:, lanes],
                corner_b[cell:, lanes],
            ],
            axis=0,
        )
        scores = lax.dot_general(
            query, keys, (((1,), (1,)), ((), ())), preferred_element_type=jnp.float32
        )
        scores = jnp.minimum(scores, cap_ref[...])
        top = jnp.max(scores, axis=1, keepdims=True)
        weights = jnp.exp2((scores - top) * (math.log2(math.e) / math.sqrt(DH)))
        total = jnp.sum(weights, axis=1, keepdims=True)
        probs = (weights * (1.0 / total)).astype(jnp.bfloat16)
        out = jnp.dot(probs, values, preferred_element_type=jnp.float32)
        out_ref[:, lanes] = out.astype(jnp.bfloat16)


def attend(pattern, query, key, value, sides, corners):
    wide = HSTEP * DH
    own = pl.BlockSpec((TOK, wide), lambda h: (0, h))
    side = pl.BlockSpec((2, EDGE, wide), lambda h: (0, 0, h))
    corner = pl.BlockSpec((EDGE, wide), lambda h: (0, h))
    return pl.pallas_call(
        attend_kernel,
        out_shape=jax.ShapeDtypeStruct((TOK, FEAT), jnp.bfloat16),
        grid=(HEADS // HSTEP,),
        in_specs=[
            pl.BlockSpec(memory_space=pltpu.SMEM),
            pl.BlockSpec((8, NKEY), lambda h: (0, 0)),
            own,
            own,
            own,
        ]
        + [side] * 4
        + [corner] * 4,
        out_specs=own,
        scratch_shapes=[pltpu.VMEM((TOK, NKEY), jnp.float32)],
        cost_estimate=pl.CostEstimate(
            flops=4 * HEADS * TOK * NKEY * DH,
            bytes_accessed=2 * FEAT * (2 * TOK + 2 * NKEY),
            transcendentals=HEADS * TOK * NKEY,
        ),
        name="attend",
    )(pattern, jnp.asarray(key_block_ids()), query, key, value, *sides, *corners)


def shift(x, axis, step):
    count = lax.axis_size(axis)
    if step > 0:
        pairs = [(i, i + 1) for i in range(count - 1)]
    else:
        pairs = [(i + 1, i) for i in range(count - 1)]
    return lax.ppermute(x, axis, pairs)


def edges(key, value):
    def flat(cut):
        return jnp.stack([cut(x).reshape(EDGE, FEAT) for x in (key, value)])

    return (
        flat(lambda x: x[TILE - BS :]),
        flat(lambda x: x[:BS]),
        flat(lambda x: x[:, TILE - BS :]),
        flat(lambda x: x[:, :BS]),
    )


def sides_of(low, high, right, left):
    return (
        shift(low, "py", 1), shift(high, "py", -1), shift(right, "px", 1), shift(left, "px", -1)
    )


def corners_of(above, below, left, right):
    def columns(lo):
        cuts = [
            x[0].reshape(BS, TILE, FEAT)[:, lo : lo + BS].reshape(BS * BS, FEAT)
            for x in (above, below)
        ]
        return jnp.concatenate(cuts, axis=0)

    def rows(lo):
        return jnp.concatenate([x[1, lo * BS : lo * BS + BS * BS] for x in (left, right)], axis=0)

    return (
        shift(columns(TILE - BS), "px", 1),
        shift(columns(0), "px", -1),
        shift(rows(TILE - BS), "py", 1),
        shift(rows(0), "py", -1),
    )


def exchange(x, axis):
    return lax.all_to_all(x, axis, 0, 0)


def everyone(x, axis, count):
    return exchange(jnp.broadcast_to(x[None], (count,) + x.shape), axis)


def per_device(queries, keys, values, pattern, targets, router_q, router_k):
    tiles_y, tiles_x = lax.axis_size("py"), lax.axis_size("px")
    tiles = tiles_y * tiles_x
    normal = float(TOPK * HEADS * 4 * tiles)
    query, key, value = (x[0].reshape(TOK, FEAT) for x in (queries, keys, values))
    pat = pattern.reshape(4, NOFF)
    aim = targets.reshape(4, HEADS, TOPK).transpose(1, 0, 2)
    aux = jnp.concatenate([jnp.broadcast_to(pat, (HEADS, 4, NOFF)), aim], axis=2)
    aux = jnp.pad(aux.astype(jnp.float32), ((0, 0), (0, 4), (0, DH - NOFF - TOPK)))

    sent = pool(query, key, aux)
    recv = exchange(sent, TILES)
    rims = edges(keys[0], values[0])
    sides = sides_of(*rims)
    me = lax.axis_index("py") * tiles_x + lax.axis_index("px")
    head = jnp.minimum(me, HEADS - 1).astype(jnp.int32).reshape(1)
    grads = router_grads(
        head, recv, router_q.swapaxes(1, 2), router_k.swapaxes(1, 2), normal
    )
    near = lax.axis_size("x") * lax.axis_size("core")
    rows = 2 * RW // near
    parts = exchange(grads.reshape(near, rows, DH), NEAR)
    part = jnp.sum(parts, axis=0)
    far = everyone(part, "far", lax.axis_size("far"))
    part = jnp.sum(far, axis=0).astype(jnp.bfloat16)
    heads = everyone(part, TILES, tiles)
    every = everyone(heads, NEAR, near)[:, :HEADS].astype(jnp.float32)
    every = every.transpose(1, 0, 2, 3).reshape(HEADS, 2 * RW, DH)
    grad_q, grad_k = (x.swapaxes(1, 2) for x in (every[:, :RW], every[:, RW:]))
    corners = corners_of(*sides)
    attended = attend(pat, query, key, value, sides, corners)
    return (attended.reshape(1, TILE, TILE, FEAT), grad_q, grad_k)


def solution(mesh):
    sizes = IMG_SIZES if mesh.shape["img"] == math.prod(IMG_SIZES) else (1, 1, mesh.shape["img"])
    split = Mesh(mesh.devices.reshape(sizes + mesh.devices.shape[1:]), IMG + TILES)
    return jax.shard_map(
        per_device,
        mesh=split,
        in_specs=(
            P(IMG, "py", "px", None),
            P(IMG, "py", "px", None),
            P(IMG, "py", "px", None),
            P(IMG, "py", "px", None),
            P(IMG, "py", "px", None, None),
            P(),
            P(),
        ),
        out_specs=(P(IMG, "py", "px", None), P(), P()),
        check_vma=False,
    )
```

```python
import functools
import math

import jax
import jax.numpy as jnp
import numpy as np
from jax import lax
from jax.experimental import pallas as pl
from jax.experimental.pallas import tpu as pltpu
from jax.sharding import Mesh
from jax.sharding import PartitionSpec as P

HEADS = 12
DH = 128
RW = 64
BS = 8
TOPK = 3
NOFF = 9
TILE = 16
TOK = TILE * TILE
FEAT = HEADS * DH
EDGE = BS * TILE
NKEY = TOK + 6 * EDGE
SLOTS = 16
AIM_LANE = 16
CUT = 512
HSTEP = 2
LIVE_CAP = 3.4e38
DEAD_CAP = -1e30
TILES = ("py", "px")
NEAR = ("x", "core")
IMG = ("x", "far", "core")
IMG_SIZES = (4, 4, 2)


def key_block_ids():
    ids = np.zeros((8, NKEY), np.int32)
    own = np.arange(TOK)
    row = [(1 + own // TILE // BS) * 4 + 1 + own % TILE // BS]
    edge = np.arange(EDGE)
    row.append(1 + edge % TILE // BS)
    row.append(12 + 1 + edge % TILE // BS)
    row.append((1 + edge // BS // BS) * 4)
    row.append((1 + edge // BS // BS) * 4 + 3)
    row.append(edge // (BS * BS) * 12)
    row.append(edge // (BS * BS) * 12 + 3)
    ids[:] = np.concatenate(row)[None]
    return ids


def pool_kernel(pat_ref, aim_ref, q_ref, k_ref, out_ref, aux_ref):
    row = lax.broadcasted_iota(jnp.int32, (8, TOK), 0)
    tok = lax.broadcasted_iota(jnp.int32, (8, TOK), 1)
    block = tok // TILE // BS * 2 + tok % TILE // BS
    pick_q = (row == block).astype(jnp.float32).astype(jnp.bfloat16)
    pick_k = (row == block + 4).astype(jnp.float32).astype(jnp.bfloat16)
    sums = jnp.dot(pick_q, q_ref[...], preferred_element_type=jnp.float32)
    sums += jnp.dot(pick_k, k_ref[...], preferred_element_type=jnp.float32)
    means = sums / (BS * BS)
    aux_ref[...] = jnp.zeros((8, DH), jnp.float32)
    for y in range(2):
        aux_ref[2 * y : 2 * y + 2, 0:NOFF] = pat_ref[y].astype(jnp.float32)
        for k in range(TOPK):
            at = AIM_LANE * (k + 1)
            aux_ref[2 * y : 2 * y + 2, at : at + HEADS] = aim_ref[y, k].astype(jnp.float32)
    aux = aux_ref[...]
    for h in range(HEADS):
        out_ref[h, 0:8, :] = means[:, h * DH : (h + 1) * DH]
        out_ref[h, 8:16, :] = aux
    for h in range(HEADS, SLOTS):
        out_ref[h] = jnp.zeros((16, DH), jnp.float32)


def pool(pattern, aims, query, key):
    return pl.pallas_call(
        pool_kernel,
        out_shape=jax.ShapeDtypeStruct((SLOTS, 16, DH), jnp.float32),
        scratch_shapes=[pltpu.VMEM((8, DH), jnp.float32)],
        name="pool",
    )(pattern, aims, query, key)


def rim_kernel(k_ref, v_ref, low_ref, high_ref, right_ref, left_ref):
    for i, ref in enumerate((k_ref, v_ref)):
        wide = ref[...].astype(jnp.float32)
        lanes = wide.shape[-1]

        def flat(x):
            return x.reshape(EDGE, lanes).astype(jnp.bfloat16)

        low_ref[i] = flat(wide[TILE - BS :])
        high_ref[i] = flat(wide[:BS])
        right_ref[i] = flat(wide[:, TILE - BS :])
        left_ref[i] = flat(wide[:, :BS])


def rims_of(key, value):
    tile = pl.BlockSpec((TILE, TILE, CUT), lambda i: (0, 0, i))
    return pl.pallas_call(
        rim_kernel,
        out_shape=[jax.ShapeDtypeStruct((2, EDGE, FEAT), jnp.bfloat16)] * 4,
        grid=(FEAT // CUT,),
        in_specs=[tile, tile],
        out_specs=[pl.BlockSpec((2, EDGE, CUT), lambda i: (0, 0, i))] * 4,
        name="rims",
    )(key, value)


def corner_kernel(a_ref, b_ref, l_ref, r_ref, right_ref, left_ref, low_ref, high_ref):
    lanes = a_ref.shape[-1]
    cell = BS * BS
    for i, ref in enumerate((a_ref, b_ref)):
        wide = ref[0].astype(jnp.float32).reshape(BS, TILE, lanes)
        at = slice(i * cell, (i + 1) * cell)
        right_ref[at] = wide[:, TILE - BS :].reshape(cell, lanes).astype(jnp.bfloat16)
        left_ref[at] = wide[:, :BS].reshape(cell, lanes).astype(jnp.bfloat16)
    for i, ref in enumerate((l_ref, r_ref)):
        at = slice(i * cell, (i + 1) * cell)
        low_ref[at] = ref[0, cell:]
        high_ref[at] = ref[0, :cell]


def corner_parts(above, below, left, right):
    key_side = pl.BlockSpec((1, EDGE, CUT), lambda i: (0, 0, i))
    value_side = pl.BlockSpec((1, EDGE, CUT), lambda i: (1, 0, i))
    return pl.pallas_call(
        corner_kernel,
        out_shape=[jax.ShapeDtypeStruct((EDGE, FEAT), jnp.bfloat16)] * 4,
        grid=(FEAT // CUT,),
        in_specs=[key_side, key_side, value_side, value_side],
        out_specs=[pl.BlockSpec((EDGE, CUT), lambda i: (0, i))] * 4,
        name="corners",
    )(above, below, left, right)


def router_kernel(normal, head_ref, recv_ref, wq_ref, wk_ref, out_ref, pq_ref, pk_ref, ax_ref):
    for i in range(SLOTS):
        pq_ref[4 * i : 4 * i + 4, :] = recv_ref[i, 0:4, :]
        pk_ref[4 * i : 4 * i + 4, :] = recv_ref[i, 4:8, :]
        ax_ref[4 * i : 4 * i + 4, :] = recv_ref[i, 8:12, :]
    n = 4 * SLOTS
    dot = functools.partial(
        lax.dot_general, precision=lax.Precision.HIGHEST, preferred_element_type=jnp.float32
    )
    ab, abt, atb = (((1,), (0,)), ((), ())), (((1,), (1,)), ((), ())), (((0,), (0,)), ((), ()))
    pooled_q, pooled_k, aux = pq_ref[...], pk_ref[...], ax_ref[...]
    route_q = dot(pooled_q, wq_ref[0], abt)
    route_k = dot(pooled_k, wk_ref[0], abt)
    logits = dot(route_q, route_k, abt) / math.sqrt(RW)

    def place(i):
        tile, sub = i // 4, i % 4
        return tile // 4 * 2 + sub // 2, tile % 4 * 2 + sub % 2

    qy, qx = place(lax.broadcasted_iota(jnp.int32, (n, n), 0))
    ky, kx = place(lax.broadcasted_iota(jnp.int32, (n, n), 1))
    up, left = ky - qy + 1, kx - qx + 1
    near = (up >= 0) & (up <= 2) & (left >= 0) & (left <= 2)
    off = jnp.where(near, 3 * up + left, -1).astype(jnp.float32)
    live = jnp.zeros((n, n), jnp.float32)
    for o in range(NOFF):
        live = jnp.where(off == float(o), aux[:, o : o + 1], live)
    picks = jnp.zeros((n, n), jnp.float32)
    lane = lax.broadcasted_iota(jnp.int32, (n, DH), 1)
    for k in range(TOPK):
        mine = jnp.where(lane == AIM_LANE * (k + 1) + head_ref[0], aux, 0.0)
        picks += (off == jnp.sum(mine, axis=1, keepdims=True)).astype(jnp.float32)
    logits = jnp.where(live > 0.5, logits, -1e30)
    top = jnp.max(logits, axis=1, keepdims=True)
    weights = jnp.exp(logits - top)
    soft = weights / jnp.sum(weights, axis=1, keepdims=True)
    count = jnp.sum(picks, axis=1, keepdims=True)
    slope = jnp.where(live > 0.5, count * soft - picks, 0.0) * (1.0 / (normal * math.sqrt(RW)))
    out_ref[0:RW, :] = dot(dot(slope, route_k, ab), pooled_q, atb)
    out_ref[RW:, :] = dot(dot(slope, route_q, atb), pooled_k, atb)


def router_grads(head, recv, weights_q, weights_k, normal):
    spec = pl.BlockSpec((1, RW, DH), lambda i, h: (h[0], 0, 0))
    return pl.pallas_call(
        functools.partial(router_kernel, normal),
        out_shape=jax.ShapeDtypeStruct((2 * RW, DH), jnp.float32),
        grid_spec=pltpu.PrefetchScalarGridSpec(
            num_scalar_prefetch=1,
            grid=(1,),
            in_specs=[
                pl.BlockSpec((SLOTS, 16, DH), lambda i, h: (0, 0, 0)),
                spec,
                spec,
            ],
            out_specs=pl.BlockSpec((2 * RW, DH), lambda i, h: (0, 0)),
            scratch_shapes=[pltpu.VMEM((4 * SLOTS, DH), jnp.float32)] * 3,
        ),
        name="router",
    )(head, recv, weights_q, weights_k)


def attend_kernel(pat_ref, ids_ref, q_ref, k_ref, v_ref, *rest):
    sides, (corner_l, corner_r, corner_a, corner_b, out_ref, cap_ref) = rest[:4], rest[4:]
    cell = BS * BS

    @pl.when(pl.program_id(0) == 0)
    def _():
        ids = ids_ref[...]
        tok = lax.broadcasted_iota(jnp.int32, (TOK, NKEY), 0)
        block = tok // TILE // BS * 2 + tok % TILE // BS
        cap = jnp.full((TOK, NKEY), DEAD_CAP, jnp.float32)
        for b in range(4):
            line = jnp.full((8, NKEY), DEAD_CAP, jnp.float32)
            for o in range(NOFF):
                at = (b // 2 + o // 3) * 4 + b % 2 + o % 3
                value = jnp.where(pat_ref[b, o] > 0, LIVE_CAP, DEAD_CAP)
                line = jnp.where(ids == at, value, line)
            cap = jnp.where(block == b, line[0:1, :], cap)
        cap_ref[...] = cap

    for h in range(HSTEP):
        lanes = slice(h * DH, (h + 1) * DH)
        query = q_ref[:, lanes]
        keys = jnp.concatenate(
            [k_ref[:, lanes]]
            + [s[0, :, lanes] for s in sides]
            + [corner_l[:, lanes], corner_r[:, lanes]],
            axis=0,
        )
        values = jnp.concatenate(
            [v_ref[:, lanes]]
            + [s[1, :, lanes] for s in sides]
            + [
                corner_a[:cell, lanes],
                corner_b[:cell, lanes],
                corner_a[cell:, lanes],
                corner_b[cell:, lanes],
            ],
            axis=0,
        )
        scores = lax.dot_general(
            query, keys, (((1,), (1,)), ((), ())), preferred_element_type=jnp.float32
        )
        scores = jnp.minimum(scores, cap_ref[...])
        top = jnp.max(scores, axis=1, keepdims=True)
        weights = jnp.exp2((scores - top) * (math.log2(math.e) / math.sqrt(DH)))
        total = jnp.sum(weights, axis=1, keepdims=True)
        probs = (weights * (1.0 / total)).astype(jnp.bfloat16)
        out = jnp.dot(probs, values, preferred_element_type=jnp.float32)
        out_ref[:, lanes] = out.astype(jnp.bfloat16)


def attend(pattern, query, key, value, sides, corners):
    wide = HSTEP * DH
    own = pl.BlockSpec((TOK, wide), lambda h: (0, h))
    side = pl.BlockSpec((2, EDGE, wide), lambda h: (0, 0, h))
    corner = pl.BlockSpec((EDGE, wide), lambda h: (0, h))
    return pl.pallas_call(
        attend_kernel,
        out_shape=jax.ShapeDtypeStruct((TOK, FEAT), jnp.bfloat16),
        grid=(HEADS // HSTEP,),
        in_specs=[
            pl.BlockSpec(memory_space=pltpu.SMEM),
            pl.BlockSpec((8, NKEY), lambda h: (0, 0)),
            own,
            own,
            own,
        ]
        + [side] * 4
        + [corner] * 4,
        out_specs=own,
        scratch_shapes=[pltpu.VMEM((TOK, NKEY), jnp.float32)],
        cost_estimate=pl.CostEstimate(
            flops=4 * HEADS * TOK * NKEY * DH,
            bytes_accessed=2 * FEAT * (2 * TOK + 2 * NKEY),
            transcendentals=HEADS * TOK * NKEY,
        ),
        name="attend",
    )(pattern, jnp.asarray(key_block_ids()), query, key, value, *sides, *corners)


def shift(x, axis, step):
    count = lax.axis_size(axis)
    if step > 0:
        pairs = [(i, i + 1) for i in range(count - 1)]
    else:
        pairs = [(i + 1, i) for i in range(count - 1)]
    return lax.ppermute(x, axis, pairs)


def sides_of(low, high, right, left):
    return (
        shift(low, "py", 1), shift(high, "py", -1), shift(right, "px", 1), shift(left, "px", -1)
    )


def corners_of(above, below, left, right):
    to_right, to_left, to_low, to_high = corner_parts(above, below, left, right)
    return (
        shift(to_right, "px", 1),
        shift(to_left, "px", -1),
        shift(to_low, "py", 1),
        shift(to_high, "py", -1),
    )


def exchange(x, axis):
    return lax.all_to_all(x, axis, 0, 0)


def everyone(x, axis, count):
    return exchange(jnp.broadcast_to(x[None], (count,) + x.shape), axis)


def per_device(queries, keys, values, pattern, targets, router_q, router_k):
    tiles_y, tiles_x = lax.axis_size("py"), lax.axis_size("px")
    tiles = tiles_y * tiles_x
    normal = float(TOPK * HEADS * 4 * tiles)
    query, key, value = (x[0].reshape(TOK, FEAT) for x in (queries, keys, values))
    aims = targets[0].transpose(0, 3, 1, 2)
    sent = pool(pattern[0], aims, query, key)
    recv = exchange(sent, TILES)
    sides = sides_of(*rims_of(keys[0], values[0]))
    me = lax.axis_index("py") * tiles_x + lax.axis_index("px")
    head = jnp.minimum(me, HEADS - 1).astype(jnp.int32).reshape(1)
    grads = router_grads(
        head, recv, router_q.swapaxes(1, 2), router_k.swapaxes(1, 2), normal
    )
    near = lax.axis_size("x") * lax.axis_size("core")
    rows = 2 * RW // near
    parts = exchange(grads.reshape(near, rows, DH), NEAR)
    part = jnp.sum(parts, axis=0)
    far = everyone(part, "far", lax.axis_size("far"))
    part = jnp.sum(far, axis=0).astype(jnp.bfloat16)
    heads = everyone(part, TILES, tiles)
    every = everyone(heads, NEAR, near)[:, :HEADS].astype(jnp.float32)
    every = every.transpose(1, 0, 2, 3).reshape(HEADS, 2 * RW, DH)
    grad_q, grad_k = (x.swapaxes(1, 2) for x in (every[:, :RW], every[:, RW:]))
    corners = corners_of(*sides)
    attended = attend(pattern.reshape(4, NOFF), query, key, value, sides, corners)
    return (attended.reshape(1, TILE, TILE, FEAT), grad_q, grad_k)


def solution(mesh):
    sizes = IMG_SIZES if mesh.shape["img"] == math.prod(IMG_SIZES) else (1, 1, mesh.shape["img"])
    split = Mesh(mesh.devices.reshape(sizes + mesh.devices.shape[1:]), IMG + TILES)
    return jax.shard_map(
        per_device,
        mesh=split,
        in_specs=(
            P(IMG, "py", "px", None),
            P(IMG, "py", "px", None),
            P(IMG, "py", "px", None),
            P(IMG, "py", "px", None),
            P(IMG, "py", "px", None, None),
            P(),
            P(),
        ),
        out_specs=(P(IMG, "py", "px", None), P(), P()),
        check_vma=False,
    )
```

```python
import functools
import math

import jax
import jax.numpy as jnp
import numpy as np
from jax import lax
from jax.experimental import pallas as pl
from jax.experimental.pallas import tpu as pltpu
from jax.sharding import Mesh
from jax.sharding import PartitionSpec as P

HEADS = 12
DH = 128
RW = 64
BS = 8
TOPK = 3
NOFF = 9
TILE = 16
TOK = TILE * TILE
FEAT = HEADS * DH
EDGE = BS * TILE
NKEY = TOK + 6 * EDGE
SLOTS = 16
AIM_LANE = 16
PSTEP = 4
CUT = 768
HSTEP = 2
LIVE_CAP = 3.4e38
DEAD_CAP = -1e30
TILES = ("py", "px")
NEAR = ("x", "core")
IMG = ("x", "far", "core")
IMG_SIZES = (4, 4, 2)


def key_block_ids():
    ids = np.zeros((8, NKEY), np.int32)
    own = np.arange(TOK)
    row = [(1 + own // TILE // BS) * 4 + 1 + own % TILE // BS]
    edge = np.arange(EDGE)
    row.append(1 + edge % TILE // BS)
    row.append(12 + 1 + edge % TILE // BS)
    row.append((1 + edge // BS // BS) * 4)
    row.append((1 + edge // BS // BS) * 4 + 3)
    row.append(edge // (BS * BS) * 3)
    row.append(edge // (BS * BS) * 3 + 12)
    ids[:] = np.concatenate(row)[None]
    return ids


def pool_kernel(pat_ref, aim_ref, q_ref, k_ref, out_ref, aux_ref):
    step = pl.program_id(0)

    @pl.when(step == 0)
    def _():
        aux_ref[...] = jnp.zeros((8, DH), jnp.float32)
        for y in range(2):
            aux_ref[2 * y : 2 * y + 2, 0:NOFF] = pat_ref[y].astype(jnp.float32)
            for k in range(TOPK):
                at = AIM_LANE * (k + 1)
                aux_ref[2 * y : 2 * y + 2, at : at + HEADS] = aim_ref[y, k].astype(jnp.float32)

    @pl.when(step < HEADS // PSTEP)
    def _():
        row = lax.broadcasted_iota(jnp.int32, (8, TOK), 0)
        tok = lax.broadcasted_iota(jnp.int32, (8, TOK), 1)
        block = tok // TILE // BS * 2 + tok % TILE // BS
        pick_q = (row == block).astype(jnp.float32).astype(jnp.bfloat16)
        pick_k = (row == block + 4).astype(jnp.float32).astype(jnp.bfloat16)
        sums = jnp.dot(pick_q, q_ref[...], preferred_element_type=jnp.float32)
        sums += jnp.dot(pick_k, k_ref[...], preferred_element_type=jnp.float32)
        means = sums / (BS * BS)
        for h in range(PSTEP):
            out_ref[h, 0:8, :] = means[:, h * DH : (h + 1) * DH]
            out_ref[h, 8:16, :] = aux_ref[...]

    @pl.when(step >= HEADS // PSTEP)
    def _():
        out_ref[...] = jnp.zeros((PSTEP, 16, DH), jnp.float32)


def pool(pattern, aims, query, key):
    last = HEADS // PSTEP - 1
    tile = pl.BlockSpec((TOK, PSTEP * DH), lambda i: (0, jnp.minimum(i, last)))
    return pl.pallas_call(
        pool_kernel,
        out_shape=jax.ShapeDtypeStruct((SLOTS, 16, DH), jnp.float32),
        grid=(SLOTS // PSTEP,),
        in_specs=[
            pl.BlockSpec(pattern.shape, lambda i: (0, 0, 0)),
            pl.BlockSpec(aims.shape, lambda i: (0, 0, 0, 0)),
            tile,
            tile,
        ],
        out_specs=pl.BlockSpec((PSTEP, 16, DH), lambda i: (i, 0, 0)),
        scratch_shapes=[pltpu.VMEM((8, DH), jnp.float32)],
        name="pool",
    )(pattern, aims, query, key)


def rim_kernel(k_ref, v_ref, low_ref, high_ref, right_ref, left_ref):
    for i, ref in enumerate((k_ref, v_ref)):
        wide = ref[...].astype(jnp.float32)
        lanes = wide.shape[-1]

        def flat(x):
            return x.reshape(EDGE, lanes).astype(jnp.bfloat16)

        low_ref[i] = flat(wide[TILE - BS :])
        high_ref[i] = flat(wide[:BS])
        right_ref[i] = flat(wide[:, TILE - BS :])
        left_ref[i] = flat(wide[:, :BS])


def rims_of(key, value):
    tile = pl.BlockSpec((TILE, TILE, CUT), lambda i: (0, 0, i))
    return pl.pallas_call(
        rim_kernel,
        out_shape=[jax.ShapeDtypeStruct((2, EDGE, FEAT), jnp.bfloat16)] * 4,
        grid=(FEAT // CUT,),
        in_specs=[tile, tile],
        out_specs=[pl.BlockSpec((2, EDGE, CUT), lambda i: (0, 0, i))] * 4,
        name="rims",
    )(key, value)


def corner_kernel(l_ref, r_ref, low_ref, high_ref):
    cell = BS * BS
    for i, ref in enumerate((l_ref, r_ref)):
        at = slice(i * cell, (i + 1) * cell)
        low_ref[:, at] = ref[:, cell:]
        high_ref[:, at] = ref[:, :cell]


def corner_parts(left, right):
    side = pl.BlockSpec((2, EDGE, CUT), lambda i: (0, 0, i))
    return pl.pallas_call(
        corner_kernel,
        out_shape=[jax.ShapeDtypeStruct((2, EDGE, FEAT), jnp.bfloat16)] * 2,
        grid=(FEAT // CUT,),
        in_specs=[side] * 2,
        out_specs=[side] * 2,
        name="corners",
    )(left, right)


def router_kernel(normal, head_ref, recv_ref, wq_ref, wk_ref, out_ref, pq_ref, pk_ref, ax_ref):
    for i in range(SLOTS):
        pq_ref[4 * i : 4 * i + 4, :] = recv_ref[i, 0:4, :]
        pk_ref[4 * i : 4 * i + 4, :] = recv_ref[i, 4:8, :]
        ax_ref[4 * i : 4 * i + 4, :] = recv_ref[i, 8:12, :]
    n = 4 * SLOTS
    dot = functools.partial(
        lax.dot_general, precision=lax.Precision.HIGHEST, preferred_element_type=jnp.float32
    )
    ab, abt, atb = (((1,), (0,)), ((), ())), (((1,), (1,)), ((), ())), (((0,), (0,)), ((), ()))
    pooled_q, pooled_k, aux = pq_ref[...], pk_ref[...], ax_ref[...]
    route_q = dot(pooled_q, wq_ref[0], abt)
    route_k = dot(pooled_k, wk_ref[0], abt)
    logits = dot(route_q, route_k, abt) / math.sqrt(RW)

    def place(i):
        tile, sub = i // 4, i % 4
        return tile // 4 * 2 + sub // 2, tile % 4 * 2 + sub % 2

    qy, qx = place(lax.broadcasted_iota(jnp.int32, (n, n), 0))
    ky, kx = place(lax.broadcasted_iota(jnp.int32, (n, n), 1))
    up, left = ky - qy + 1, kx - qx + 1
    near = (up >= 0) & (up <= 2) & (left >= 0) & (left <= 2)
    off = jnp.where(near, 3 * up + left, -1).astype(jnp.float32)
    live = jnp.zeros((n, n), jnp.float32)
    for o in range(NOFF):
        live = jnp.where(off == float(o), aux[:, o : o + 1], live)
    picks = jnp.zeros((n, n), jnp.float32)
    lane = lax.broadcasted_iota(jnp.int32, (n, DH), 1)
    for k in range(TOPK):
        mine = jnp.where(lane == AIM_LANE * (k + 1) + head_ref[0], aux, 0.0)
        picks += (off == jnp.sum(mine, axis=1, keepdims=True)).astype(jnp.float32)
    logits = jnp.where(live > 0.5, logits, -1e30)
    top = jnp.max(logits, axis=1, keepdims=True)
    weights = jnp.exp(logits - top)
    soft = weights / jnp.sum(weights, axis=1, keepdims=True)
    count = jnp.sum(picks, axis=1, keepdims=True)
    slope = jnp.where(live > 0.5, count * soft - picks, 0.0) * (1.0 / (normal * math.sqrt(RW)))
    out_ref[0:RW, :] = dot(dot(slope, route_k, ab), pooled_q, atb)
    out_ref[RW:, :] = dot(dot(slope, route_q, atb), pooled_k, atb)


def router_grads(head, recv, weights_q, weights_k, normal):
    spec = pl.BlockSpec((1, RW, DH), lambda i, h: (h[0], 0, 0))
    return pl.pallas_call(
        functools.partial(router_kernel, normal),
        out_shape=jax.ShapeDtypeStruct((2 * RW, DH), jnp.float32),
        grid_spec=pltpu.PrefetchScalarGridSpec(
            num_scalar_prefetch=1,
            grid=(1,),
            in_specs=[
                pl.BlockSpec((SLOTS, 16, DH), lambda i, h: (0, 0, 0)),
                spec,
                spec,
            ],
            out_specs=pl.BlockSpec((2 * RW, DH), lambda i, h: (0, 0)),
            scratch_shapes=[pltpu.VMEM((4 * SLOTS, DH), jnp.float32)] * 3,
        ),
        name="router",
    )(head, recv, weights_q, weights_k)


def attend_kernel(pat_ref, ids_ref, q_ref, k_ref, v_ref, *rest):
    sides, (out_ref, cap_ref) = rest[:6], rest[6:]

    @pl.when(pl.program_id(0) == 0)
    def _():
        ids = ids_ref[...]
        tok = lax.broadcasted_iota(jnp.int32, (TOK, NKEY), 0)
        block = tok // TILE // BS * 2 + tok % TILE // BS
        cap = jnp.full((TOK, NKEY), DEAD_CAP, jnp.float32)
        for b in range(4):
            line = jnp.full((8, NKEY), DEAD_CAP, jnp.float32)
            for o in range(NOFF):
                at = (b // 2 + o // 3) * 4 + b % 2 + o % 3
                value = jnp.where(pat_ref[b, o] > 0, LIVE_CAP, DEAD_CAP)
                line = jnp.where(ids == at, value, line)
            cap = jnp.where(block == b, line[0:1, :], cap)
        cap_ref[...] = cap

    for h in range(HSTEP):
        lanes = slice(h * DH, (h + 1) * DH)
        query = q_ref[:, lanes]
        keys = jnp.concatenate([k_ref[:, lanes]] + [s[0, :, lanes] for s in sides], axis=0)
        values = jnp.concatenate([v_ref[:, lanes]] + [s[1, :, lanes] for s in sides], axis=0)
        scores = lax.dot_general(
            query, keys, (((1,), (1,)), ((), ())), preferred_element_type=jnp.float32
        )
        scores = jnp.minimum(scores, cap_ref[...])
        top = jnp.max(scores, axis=1, keepdims=True)
        weights = jnp.exp2((scores - top) * (math.log2(math.e) / math.sqrt(DH)))
        total = jnp.sum(weights, axis=1, keepdims=True)
        probs = (weights * (1.0 / total)).astype(jnp.bfloat16)
        out = jnp.dot(probs, values, preferred_element_type=jnp.float32)
        out_ref[:, lanes] = out.astype(jnp.bfloat16)


def attend(pattern, query, key, value, sides):
    wide = HSTEP * DH
    own = pl.BlockSpec((TOK, wide), lambda h: (0, h))
    side = pl.BlockSpec((2, EDGE, wide), lambda h: (0, 0, h))
    return pl.pallas_call(
        attend_kernel,
        out_shape=jax.ShapeDtypeStruct((TOK, FEAT), jnp.bfloat16),
        grid=(HEADS // HSTEP,),
        in_specs=[
            pl.BlockSpec(memory_space=pltpu.SMEM),
            pl.BlockSpec((8, NKEY), lambda h: (0, 0)),
            own,
            own,
            own,
        ]
        + [side] * 6,
        out_specs=own,
        scratch_shapes=[pltpu.VMEM((TOK, NKEY), jnp.float32)],
        cost_estimate=pl.CostEstimate(
            flops=4 * HEADS * TOK * NKEY * DH,
            bytes_accessed=2 * FEAT * (2 * TOK + 2 * NKEY),
            transcendentals=HEADS * TOK * NKEY,
        ),
        name="attend",
    )(pattern, jnp.asarray(key_block_ids()), query, key, value, *sides)


def shift(x, axis, step):
    count = lax.axis_size(axis)
    if step > 0:
        pairs = [(i, i + 1) for i in range(count - 1)]
    else:
        pairs = [(i + 1, i) for i in range(count - 1)]
    return lax.ppermute(x, axis, pairs)


def sides_of(low, high, right, left):
    return (
        shift(low, "py", 1), shift(high, "py", -1), shift(right, "px", 1), shift(left, "px", -1)
    )


def corners_of(left, right):
    low, high = corner_parts(left, right)
    return shift(low, "py", 1), shift(high, "py", -1)


def exchange(x, axis):
    return lax.all_to_all(x, axis, 0, 0)


def everyone(x, axis, count):
    return exchange(jnp.broadcast_to(x[None], (count,) + x.shape), axis)


def per_device(queries, keys, values, pattern, targets, router_q, router_k):
    tiles_y, tiles_x = lax.axis_size("py"), lax.axis_size("px")
    tiles = tiles_y * tiles_x
    normal = float(TOPK * HEADS * 4 * tiles)
    query, key, value = (x[0].reshape(TOK, FEAT) for x in (queries, keys, values))
    aims = targets[0].transpose(0, 3, 1, 2)
    sent = pool(pattern[0], aims, query, key)
    recv = exchange(sent, TILES)
    sides = sides_of(*rims_of(keys[0], values[0]))
    me = lax.axis_index("py") * tiles_x + lax.axis_index("px")
    head = jnp.minimum(me, HEADS - 1).astype(jnp.int32).reshape(1)
    grads = router_grads(
        head, recv, router_q.swapaxes(1, 2), router_k.swapaxes(1, 2), normal
    )
    near = lax.axis_size("x") * lax.axis_size("core")
    rows = 2 * RW // near
    parts = exchange(grads.reshape(near, rows, DH), NEAR)
    part = jnp.sum(parts, axis=0)
    far = everyone(part, "far", lax.axis_size("far"))
    part = jnp.sum(far, axis=0).astype(jnp.bfloat16)
    heads = everyone(part, TILES, tiles)
    every = everyone(heads, NEAR, near)[:, :HEADS].astype(jnp.float32)
    every = every.transpose(1, 0, 2, 3).reshape(HEADS, 2 * RW, DH)
    grad_q, grad_k = (x.swapaxes(1, 2) for x in (every[:, :RW], every[:, RW:]))
    corners = corners_of(*sides[2:])
    attended = attend(pattern.reshape(4, NOFF), query, key, value, sides + corners)
    return (attended.reshape(1, TILE, TILE, FEAT), grad_q, grad_k)


def solution(mesh):
    sizes = IMG_SIZES if mesh.shape["img"] == math.prod(IMG_SIZES) else (1, 1, mesh.shape["img"])
    split = Mesh(mesh.devices.reshape(sizes + mesh.devices.shape[1:]), IMG + TILES)
    return jax.shard_map(
        per_device,
        mesh=split,
        in_specs=(
            P(IMG, "py", "px", None),
            P(IMG, "py", "px", None),
            P(IMG, "py", "px", None),
            P(IMG, "py", "px", None),
            P(IMG, "py", "px", None, None),
            P(),
            P(),
        ),
        out_specs=(P(IMG, "py", "px", None), P(), P()),
        check_vma=False,
    )
```

```python
import functools
import math

import jax
import jax.numpy as jnp
import numpy as np
from jax import lax
from jax.experimental import pallas as pl
from jax.experimental.pallas import tpu as pltpu
from jax.sharding import Mesh
from jax.sharding import PartitionSpec as P

HEADS = 12
DH = 128
RW = 64
BS = 8
TOPK = 3
NOFF = 9
TILE = 16
TOK = TILE * TILE
FEAT = HEADS * DH
EDGE = BS * TILE
NKEY = TOK + 6 * EDGE
SLOTS = 16
AIM_LANE = 16
CUT = 768
HSTEP = 2
LIVE_CAP = 3.4e38
DEAD_CAP = -1e30
TILES = ("py", "px")
NEAR = ("x", "core")
IMG = ("x", "far", "core")
IMG_SIZES = (4, 4, 2)


def key_block_ids():
    ids = np.zeros((8, NKEY), np.int32)
    own = np.arange(TOK)
    row = [(1 + own // TILE // BS) * 4 + 1 + own % TILE // BS]
    edge = np.arange(EDGE)
    row.append(1 + edge % TILE // BS)
    row.append(12 + 1 + edge % TILE // BS)
    row.append((1 + edge // BS // BS) * 4)
    row.append((1 + edge // BS // BS) * 4 + 3)
    row.append(edge // (BS * BS) * 3)
    row.append(edge // (BS * BS) * 3 + 12)
    ids[:] = np.concatenate(row)[None]
    return ids


def pool_kernel(pat_ref, aim_ref, q_ref, k_ref, out_ref, aux_ref):
    row = lax.broadcasted_iota(jnp.int32, (8, TOK), 0)
    tok = lax.broadcasted_iota(jnp.int32, (8, TOK), 1)
    block = tok // TILE // BS * 2 + tok % TILE // BS
    pick_q = (row == block).astype(jnp.float32).astype(jnp.bfloat16)
    pick_k = (row == block + 4).astype(jnp.float32).astype(jnp.bfloat16)
    sums = jnp.dot(pick_q, q_ref[...], preferred_element_type=jnp.float32)
    sums += jnp.dot(pick_k, k_ref[...], preferred_element_type=jnp.float32)
    means = sums / (BS * BS)
    aux_ref[...] = jnp.zeros((8, DH), jnp.float32)
    for y in range(2):
        aux_ref[2 * y : 2 * y + 2, 0:NOFF] = pat_ref[y].astype(jnp.float32)
        for k in range(TOPK):
            at = AIM_LANE * (k + 1)
            aux_ref[2 * y : 2 * y + 2, at : at + HEADS] = aim_ref[y, k].astype(jnp.float32)
    aux = aux_ref[...]
    for h in range(HEADS):
        out_ref[h, 0:8, :] = means[:, h * DH : (h + 1) * DH]
        out_ref[h, 8:16, :] = aux
    for h in range(HEADS, SLOTS):
        out_ref[h] = jnp.zeros((16, DH), jnp.float32)


def pool(pattern, aims, query, key):
    return pl.pallas_call(
        pool_kernel,
        out_shape=jax.ShapeDtypeStruct((SLOTS, 16, DH), jnp.float32),
        scratch_shapes=[pltpu.VMEM((8, DH), jnp.float32)],
        name="pool",
    )(pattern, aims, query, key)


def rim_kernel(k_ref, v_ref, low_ref, high_ref, right_ref, left_ref):
    for i, ref in enumerate((k_ref, v_ref)):
        wide = ref[...].astype(jnp.float32)
        lanes = wide.shape[-1]

        def flat(x):
            return x.reshape(EDGE, lanes).astype(jnp.bfloat16)

        low_ref[i] = flat(wide[TILE - BS :])
        high_ref[i] = flat(wide[:BS])
        right_ref[i] = flat(wide[:, TILE - BS :])
        left_ref[i] = flat(wide[:, :BS])


def rims_of(key, value):
    tile = pl.BlockSpec((TILE, TILE, CUT), lambda i: (0, 0, i))
    return pl.pallas_call(
        rim_kernel,
        out_shape=[jax.ShapeDtypeStruct((2, EDGE, FEAT), jnp.bfloat16)] * 4,
        grid=(FEAT // CUT,),
        in_specs=[tile, tile],
        out_specs=[pl.BlockSpec((2, EDGE, CUT), lambda i: (0, 0, i))] * 4,
        name="rims",
    )(key, value)


def corner_kernel(l_ref, r_ref, low_ref, high_ref):
    cell = BS * BS
    for i, ref in enumerate((l_ref, r_ref)):
        at = slice(i * cell, (i + 1) * cell)
        low_ref[:, at] = ref[:, cell:]
        high_ref[:, at] = ref[:, :cell]


def corner_parts(left, right):
    side = pl.BlockSpec((2, EDGE, CUT), lambda i: (0, 0, i))
    return pl.pallas_call(
        corner_kernel,
        out_shape=[jax.ShapeDtypeStruct((2, EDGE, FEAT), jnp.bfloat16)] * 2,
        grid=(FEAT // CUT,),
        in_specs=[side] * 2,
        out_specs=[side] * 2,
        name="corners",
    )(left, right)


def router_kernel(normal, head_ref, recv_ref, wq_ref, wk_ref, out_ref, pq_ref, pk_ref, ax_ref):
    for i in range(SLOTS):
        pq_ref[4 * i : 4 * i + 4, :] = recv_ref[i, 0:4, :]
        pk_ref[4 * i : 4 * i + 4, :] = recv_ref[i, 4:8, :]
        ax_ref[4 * i : 4 * i + 4, :] = recv_ref[i, 8:12, :]
    n = 4 * SLOTS
    dot = functools.partial(
        lax.dot_general, precision=lax.Precision.HIGHEST, preferred_element_type=jnp.float32
    )
    ab, abt, atb = (((1,), (0,)), ((), ())), (((1,), (1,)), ((), ())), (((0,), (0,)), ((), ()))
    pooled_q, pooled_k, aux = pq_ref[...], pk_ref[...], ax_ref[...]
    route_q = dot(pooled_q, wq_ref[0], abt)
    route_k = dot(pooled_k, wk_ref[0], abt)
    logits = dot(route_q, route_k, abt) / math.sqrt(RW)

    def place(i):
        tile, sub = i // 4, i % 4
        return tile // 4 * 2 + sub // 2, tile % 4 * 2 + sub % 2

    qy, qx = place(lax.broadcasted_iota(jnp.int32, (n, n), 0))
    ky, kx = place(lax.broadcasted_iota(jnp.int32, (n, n), 1))
    up, left = ky - qy + 1, kx - qx + 1
    near = (up >= 0) & (up <= 2) & (left >= 0) & (left <= 2)
    off = jnp.where(near, 3 * up + left, -1).astype(jnp.float32)
    live = jnp.zeros((n, n), jnp.float32)
    for o in range(NOFF):
        live = jnp.where(off == float(o), aux[:, o : o + 1], live)
    picks = jnp.zeros((n, n), jnp.float32)
    lane = lax.broadcasted_iota(jnp.int32, (n, DH), 1)
    for k in range(TOPK):
        mine = jnp.where(lane == AIM_LANE * (k + 1) + head_ref[0], aux, 0.0)
        picks += (off == jnp.sum(mine, axis=1, keepdims=True)).astype(jnp.float32)
    logits = jnp.where(live > 0.5, logits, -1e30)
    top = jnp.max(logits, axis=1, keepdims=True)
    weights = jnp.exp(logits - top)
    soft = weights / jnp.sum(weights, axis=1, keepdims=True)
    count = jnp.sum(picks, axis=1, keepdims=True)
    slope = jnp.where(live > 0.5, count * soft - picks, 0.0) * (1.0 / (normal * math.sqrt(RW)))
    out_ref[0:RW, :] = dot(dot(slope, route_k, ab), pooled_q, atb)
    out_ref[RW:, :] = dot(dot(slope, route_q, atb), pooled_k, atb)


def router_grads(head, recv, weights_q, weights_k, normal):
    spec = pl.BlockSpec((1, RW, DH), lambda i, h: (h[0], 0, 0))
    return pl.pallas_call(
        functools.partial(router_kernel, normal),
        out_shape=jax.ShapeDtypeStruct((2 * RW, DH), jnp.float32),
        grid_spec=pltpu.PrefetchScalarGridSpec(
            num_scalar_prefetch=1,
            grid=(1,),
            in_specs=[
                pl.BlockSpec((SLOTS, 16, DH), lambda i, h: (0, 0, 0)),
                spec,
                spec,
            ],
            out_specs=pl.BlockSpec((2 * RW, DH), lambda i, h: (0, 0)),
            scratch_shapes=[pltpu.VMEM((4 * SLOTS, DH), jnp.float32)] * 3,
        ),
        name="router",
    )(head, recv, weights_q, weights_k)


def attend_kernel(pat_ref, ids_ref, q_ref, k_ref, v_ref, *rest):
    sides, (out_ref, cap_ref) = rest[:6], rest[6:]

    @pl.when(pl.program_id(0) == 0)
    def _():
        ids = ids_ref[...]
        tok = lax.broadcasted_iota(jnp.int32, (TOK, NKEY), 0)
        block = tok // TILE // BS * 2 + tok % TILE // BS
        cap = jnp.full((TOK, NKEY), DEAD_CAP, jnp.float32)
        for b in range(4):
            line = jnp.full((8, NKEY), DEAD_CAP, jnp.float32)
            for o in range(NOFF):
                at = (b // 2 + o // 3) * 4 + b % 2 + o % 3
                value = jnp.where(pat_ref[b, o] > 0, LIVE_CAP, DEAD_CAP)
                line = jnp.where(ids == at, value, line)
            cap = jnp.where(block == b, line[0:1, :], cap)
        cap_ref[...] = cap

    for h in range(HSTEP):
        lanes = slice(h * DH, (h + 1) * DH)
        query = q_ref[:, lanes]
        keys = jnp.concatenate([k_ref[:, lanes]] + [s[0, :, lanes] for s in sides], axis=0)
        values = jnp.concatenate([v_ref[:, lanes]] + [s[1, :, lanes] for s in sides], axis=0)
        scores = lax.dot_general(
            query, keys, (((1,), (1,)), ((), ())), preferred_element_type=jnp.float32
        )
        scores = jnp.minimum(scores, cap_ref[...])
        top = jnp.max(scores, axis=1, keepdims=True)
        weights = jnp.exp2((scores - top) * (math.log2(math.e) / math.sqrt(DH)))
        total = jnp.sum(weights, axis=1, keepdims=True)
        probs = (weights * (1.0 / total)).astype(jnp.bfloat16)
        out = jnp.dot(probs, values, preferred_element_type=jnp.float32)
        out_ref[:, lanes] = out.astype(jnp.bfloat16)


def attend(pattern, query, key, value, sides):
    wide = HSTEP * DH
    own = pl.BlockSpec((TOK, wide), lambda h: (0, h))
    side = pl.BlockSpec((2, EDGE, wide), lambda h: (0, 0, h))
    return pl.pallas_call(
        attend_kernel,
        out_shape=jax.ShapeDtypeStruct((TOK, FEAT), jnp.bfloat16),
        grid=(HEADS // HSTEP,),
        in_specs=[
            pl.BlockSpec(memory_space=pltpu.SMEM),
            pl.BlockSpec((8, NKEY), lambda h: (0, 0)),
            own,
            own,
            own,
        ]
        + [side] * 6,
        out_specs=own,
        scratch_shapes=[pltpu.VMEM((TOK, NKEY), jnp.float32)],
        cost_estimate=pl.CostEstimate(
            flops=4 * HEADS * TOK * NKEY * DH,
            bytes_accessed=2 * FEAT * (2 * TOK + 2 * NKEY),
            transcendentals=HEADS * TOK * NKEY,
        ),
        name="attend",
    )(pattern, jnp.asarray(key_block_ids()), query, key, value, *sides)


def shift(x, axis, step):
    count = lax.axis_size(axis)
    if step > 0:
        pairs = [(i, i + 1) for i in range(count - 1)]
    else:
        pairs = [(i + 1, i) for i in range(count - 1)]
    return lax.ppermute(x, axis, pairs)


def sides_of(low, high, right, left):
    return (
        shift(low, "py", 1), shift(high, "py", -1), shift(right, "px", 1), shift(left, "px", -1)
    )


def corners_of(left, right):
    low, high = corner_parts(left, right)
    return shift(low, "py", 1), shift(high, "py", -1)


def exchange(x, axis):
    return lax.all_to_all(x, axis, 0, 0)


def everyone(x, axis, count):
    return exchange(jnp.broadcast_to(x[None], (count,) + x.shape), axis)


def per_device(queries, keys, values, pattern, targets, router_q, router_k):
    tiles_y, tiles_x = lax.axis_size("py"), lax.axis_size("px")
    tiles = tiles_y * tiles_x
    normal = float(TOPK * HEADS * 4 * tiles)
    query, key, value = (x[0].reshape(TOK, FEAT) for x in (queries, keys, values))
    aims = targets[0].transpose(0, 3, 1, 2)
    sent = pool(pattern[0], aims, query, key)
    recv = exchange(sent, TILES)
    sides = sides_of(*rims_of(keys[0], values[0]))
    me = lax.axis_index("py") * tiles_x + lax.axis_index("px")
    head = jnp.minimum(me, HEADS - 1).astype(jnp.int32).reshape(1)
    grads = router_grads(
        head, recv, router_q.swapaxes(1, 2), router_k.swapaxes(1, 2), normal
    )
    near = lax.axis_size("x") * lax.axis_size("core")
    rows = 2 * RW // near
    parts = exchange(grads.reshape(near, rows, DH), NEAR)
    part = jnp.sum(parts, axis=0)
    far = everyone(part, "far", lax.axis_size("far"))
    part = jnp.sum(far, axis=0).astype(jnp.bfloat16)
    heads = everyone(part, TILES, tiles)
    every = everyone(heads, NEAR, near)[:, :HEADS].astype(jnp.float32)
    every = every.transpose(1, 0, 2, 3).reshape(HEADS, 2 * RW, DH)
    grad_q, grad_k = (x.swapaxes(1, 2) for x in (every[:, :RW], every[:, RW:]))
    corners = corners_of(*sides[2:])
    attended = attend(pattern.reshape(4, NOFF), query, key, value, sides + corners)
    return (attended.reshape(1, TILE, TILE, FEAT), grad_q, grad_k)


def solution(mesh):
    sizes = IMG_SIZES if mesh.shape["img"] == math.prod(IMG_SIZES) else (1, 1, mesh.shape["img"])
    split = Mesh(mesh.devices.reshape(sizes + mesh.devices.shape[1:]), IMG + TILES)
    return jax.shard_map(
        per_device,
        mesh=split,
        in_specs=(
            P(IMG, "py", "px", None),
            P(IMG, "py", "px", None),
            P(IMG, "py", "px", None),
            P(IMG, "py", "px", None),
            P(IMG, "py", "px", None, None),
            P(),
            P(),
        ),
        out_specs=(P(IMG, "py", "px", None), P(), P()),
        check_vma=False,
    )
```

```python
import functools
import math

import jax
import jax.numpy as jnp
import numpy as np
from jax import lax
from jax.experimental import pallas as pl
from jax.experimental.pallas import tpu as pltpu
from jax.sharding import Mesh
from jax.sharding import PartitionSpec as P

HEADS = 12
DH = 128
RW = 64
BS = 8
TOPK = 3
NOFF = 9
TILE = 16
TOK = TILE * TILE
FEAT = HEADS * DH
EDGE = BS * TILE
NKEY = TOK + 6 * EDGE
SLOTS = 16
AIM_LANE = 16
TOTAL_LANE = 64
CUT = 768
HSTEP = 2
LIVE_CAP = 3.4e38
DEAD_CAP = -1e30
TILES = ("py", "px")
NEAR = ("x", "core")
IMG = ("x", "far", "core")
IMG_SIZES = (4, 4, 2)


def key_block_ids():
    ids = np.zeros((8, NKEY), np.int32)
    own = np.arange(TOK)
    row = [(1 + own // TILE // BS) * 4 + 1 + own % TILE // BS]
    edge = np.arange(EDGE)
    row.append(1 + edge % TILE // BS)
    row.append(12 + 1 + edge % TILE // BS)
    row.append((1 + edge // BS // BS) * 4)
    row.append((1 + edge // BS // BS) * 4 + 3)
    row.append(edge // (BS * BS) * 3)
    row.append(edge // (BS * BS) * 3 + 12)
    ids[:] = np.concatenate(row)[None]
    return ids


def pool_kernel(pat_ref, aim_ref, q_ref, k_ref, out_ref, aux_ref):
    row = lax.broadcasted_iota(jnp.int32, (8, TOK), 0)
    tok = lax.broadcasted_iota(jnp.int32, (8, TOK), 1)
    block = tok // TILE // BS * 2 + tok % TILE // BS
    pick_q = (row == block).astype(jnp.float32).astype(jnp.bfloat16)
    pick_k = (row == block + 4).astype(jnp.float32).astype(jnp.bfloat16)
    sums = jnp.dot(pick_q, q_ref[...], preferred_element_type=jnp.float32)
    sums += jnp.dot(pick_k, k_ref[...], preferred_element_type=jnp.float32)
    means = sums / (BS * BS)
    aux_ref[...] = jnp.zeros((8, DH), jnp.float32)
    for y in range(2):
        aux_ref[2 * y : 2 * y + 2, 0:NOFF] = pat_ref[y].astype(jnp.float32)
        for k in range(TOPK):
            at = AIM_LANE * (k + 1)
            aux_ref[2 * y : 2 * y + 2, at : at + HEADS] = aim_ref[y, k].astype(jnp.float32)
    aux = aux_ref[...]
    for h in range(HEADS):
        out_ref[h, 0:8, :] = means[:, h * DH : (h + 1) * DH]
        out_ref[h, 8:16, :] = aux
    for h in range(HEADS, SLOTS):
        out_ref[h] = jnp.zeros((16, DH), jnp.float32)


def pool(pattern, aims, query, key):
    return pl.pallas_call(
        pool_kernel,
        out_shape=jax.ShapeDtypeStruct((SLOTS, 16, DH), jnp.float32),
        scratch_shapes=[pltpu.VMEM((8, DH), jnp.float32)],
        name="pool",
    )(pattern, aims, query, key)


def rim_kernel(k_ref, v_ref, low_ref, high_ref, right_ref, left_ref):
    for i, ref in enumerate((k_ref, v_ref)):
        wide = ref[...].astype(jnp.float32)
        lanes = wide.shape[-1]

        def flat(x):
            return x.reshape(EDGE, lanes).astype(jnp.bfloat16)

        low_ref[i] = flat(wide[TILE - BS :])
        high_ref[i] = flat(wide[:BS])
        right_ref[i] = flat(wide[:, TILE - BS :])
        left_ref[i] = flat(wide[:, :BS])


def rims_of(key, value):
    tile = pl.BlockSpec((TILE, TILE, CUT), lambda i: (0, 0, i))
    return pl.pallas_call(
        rim_kernel,
        out_shape=[jax.ShapeDtypeStruct((2, EDGE, FEAT), jnp.bfloat16)] * 4,
        grid=(FEAT // CUT,),
        in_specs=[tile, tile],
        out_specs=[pl.BlockSpec((2, EDGE, CUT), lambda i: (0, 0, i))] * 4,
        name="rims",
    )(key, value)


def corner_kernel(l_ref, r_ref, low_ref, high_ref):
    cell = BS * BS
    for i, ref in enumerate((l_ref, r_ref)):
        at = slice(i * cell, (i + 1) * cell)
        low_ref[:, at] = ref[:, cell:]
        high_ref[:, at] = ref[:, :cell]


def corner_parts(left, right):
    side = pl.BlockSpec((2, EDGE, CUT), lambda i: (0, 0, i))
    return pl.pallas_call(
        corner_kernel,
        out_shape=[jax.ShapeDtypeStruct((2, EDGE, FEAT), jnp.bfloat16)] * 2,
        grid=(FEAT // CUT,),
        in_specs=[side] * 2,
        out_specs=[side] * 2,
        name="corners",
    )(left, right)


def router_kernel(normal, head_ref, recv_ref, wq_ref, wk_ref, out_ref, pq_ref, pk_ref, ax_ref):
    for i in range(SLOTS):
        pq_ref[4 * i : 4 * i + 4, :] = recv_ref[i, 0:4, :]
        pk_ref[4 * i : 4 * i + 4, :] = recv_ref[i, 4:8, :]
        ax_ref[4 * i : 4 * i + 4, :] = recv_ref[i, 8:12, :]
    n = 4 * SLOTS
    dot = functools.partial(
        lax.dot_general, precision=lax.Precision.HIGHEST, preferred_element_type=jnp.float32
    )
    ab, abt, atb = (((1,), (0,)), ((), ())), (((1,), (1,)), ((), ())), (((0,), (0,)), ((), ()))
    pooled_q, pooled_k, aux = pq_ref[...], pk_ref[...], ax_ref[...]
    route_q = dot(pooled_q, wq_ref[0], abt)
    route_k = dot(pooled_k, wk_ref[0], abt)
    logits = dot(route_q, route_k, abt) / math.sqrt(RW)

    def place(i):
        tile, sub = i // 4, i % 4
        return tile // 4 * 2 + sub // 2, tile % 4 * 2 + sub % 2

    qy, qx = place(lax.broadcasted_iota(jnp.int32, (n, n), 0))
    ky, kx = place(lax.broadcasted_iota(jnp.int32, (n, n), 1))
    up, left = ky - qy + 1, kx - qx + 1
    near = (up >= 0) & (up <= 2) & (left >= 0) & (left <= 2)
    off = jnp.where(near, 3 * up + left, -1).astype(jnp.float32)
    live = jnp.zeros((n, n), jnp.float32)
    for o in range(NOFF):
        live = jnp.where(off == float(o), aux[:, o : o + 1], live)
    picks = jnp.zeros((n, n), jnp.float32)
    lane = lax.broadcasted_iota(jnp.int32, (n, DH), 1)
    for k in range(TOPK):
        mine = jnp.where(lane == AIM_LANE * (k + 1) + head_ref[0], aux, 0.0)
        picks += (off == jnp.sum(mine, axis=1, keepdims=True)).astype(jnp.float32)
    logits = jnp.where(live > 0.5, logits, -1e30)
    top = jnp.max(logits, axis=1, keepdims=True)
    weights = jnp.exp(logits - top)
    soft = weights / jnp.sum(weights, axis=1, keepdims=True)
    count = jnp.sum(picks, axis=1, keepdims=True)
    slope = jnp.where(live > 0.5, count * soft - picks, 0.0) * (1.0 / (normal * math.sqrt(RW)))
    out_ref[0:RW, :] = dot(dot(slope, route_k, ab), pooled_q, atb)
    out_ref[RW:, :] = dot(dot(slope, route_q, atb), pooled_k, atb)


def router_grads(head, recv, weights_q, weights_k, normal):
    spec = pl.BlockSpec((1, RW, DH), lambda i, h: (h[0], 0, 0))
    return pl.pallas_call(
        functools.partial(router_kernel, normal),
        out_shape=jax.ShapeDtypeStruct((2 * RW, DH), jnp.float32),
        grid_spec=pltpu.PrefetchScalarGridSpec(
            num_scalar_prefetch=1,
            grid=(1,),
            in_specs=[
                pl.BlockSpec((SLOTS, 16, DH), lambda i, h: (0, 0, 0)),
                spec,
                spec,
            ],
            out_specs=pl.BlockSpec((2 * RW, DH), lambda i, h: (0, 0)),
            scratch_shapes=[pltpu.VMEM((4 * SLOTS, DH), jnp.float32)] * 3,
        ),
        name="router",
    )(head, recv, weights_q, weights_k)


def build_cap(pat_ref, ids):
    width = ids.shape[1]
    tok = lax.broadcasted_iota(jnp.int32, (TOK, width), 0)
    block = tok // TILE // BS * 2 + tok % TILE // BS
    cap = jnp.full((TOK, width), DEAD_CAP, jnp.float32)
    for b in range(4):
        line = jnp.full((8, width), DEAD_CAP, jnp.float32)
        for o in range(NOFF):
            at = (b // 2 + o // 3) * 4 + b % 2 + o % 3
            value = jnp.where(pat_ref[b, o] > 0, LIVE_CAP, DEAD_CAP)
            line = jnp.where(ids == at, value, line)
        cap = jnp.where(block == b, line[0:1, :], cap)
    return cap


def capped_scores(query, keys, cap):
    scores = lax.dot_general(
        query, keys, (((1,), (1,)), ((), ())), preferred_element_type=jnp.float32
    )
    return jnp.minimum(scores, cap)


def power(x):
    return jnp.exp2(x * (math.log2(math.e) / math.sqrt(DH)))


def attend_main_kernel(pat_ref, ids_ref, q_ref, k_ref, v_ref, *rest):
    sides, (acc_ref, stat_ref, cap_ref) = rest[:4], rest[4:]
    step = pl.program_id(0)

    @pl.when(step == 0)
    def _():
        cap_ref[...] = build_cap(pat_ref, ids_ref[...])
        stat_ref[...] = jnp.zeros((TOK, DH), jnp.float32)

    lane = lax.broadcasted_iota(jnp.int32, (TOK, DH), 1)
    for h in range(HSTEP):
        head = step * HSTEP + h
        lanes = slice(h * DH, (h + 1) * DH)
        keys = jnp.concatenate([k_ref[:, lanes]] + [s[0, :, lanes] for s in sides], axis=0)
        values = jnp.concatenate([v_ref[:, lanes]] + [s[1, :, lanes] for s in sides], axis=0)
        scores = capped_scores(q_ref[:, lanes], keys, cap_ref[...])
        top = jnp.max(scores, axis=1, keepdims=True)
        weights = power(scores - top)
        total = jnp.sum(weights, axis=1, keepdims=True)
        acc_ref[:, lanes] = jnp.dot(
            weights.astype(jnp.bfloat16), values, preferred_element_type=jnp.float32
        )
        stat = jnp.where(lane == head, top, stat_ref[...])
        stat_ref[...] = jnp.where(lane == head + TOTAL_LANE, total, stat)


def attend_rest_kernel(pat_ref, ids_ref, q_ref, acc_ref, stat_ref, a_ref, b_ref, out_ref, cap_ref):
    step = pl.program_id(0)

    @pl.when(step == 0)
    def _():
        cap_ref[...] = build_cap(pat_ref, ids_ref[...])

    lane = lax.broadcasted_iota(jnp.int32, (TOK, DH), 1)
    for h in range(HSTEP):
        head = step * HSTEP + h
        lanes = slice(h * DH, (h + 1) * DH)
        keys = jnp.concatenate([s[0, :, lanes] for s in (a_ref, b_ref)], axis=0)
        values = jnp.concatenate([s[1, :, lanes] for s in (a_ref, b_ref)], axis=0)
        stat = stat_ref[...]
        main_top = jnp.sum(jnp.where(lane == head, stat, 0.0), axis=1, keepdims=True)
        main_total = jnp.sum(jnp.where(lane == head + TOTAL_LANE, stat, 0.0), axis=1, keepdims=True)
        scores = capped_scores(q_ref[:, lanes], keys, cap_ref[...])
        top = jnp.maximum(main_top, jnp.max(scores, axis=1, keepdims=True))
        weights = power(scores - top)
        keep = power(main_top - top)
        total = main_total * keep + jnp.sum(weights, axis=1, keepdims=True)
        out = acc_ref[:, lanes] * keep + jnp.dot(
            weights.astype(jnp.bfloat16), values, preferred_element_type=jnp.float32
        )
        out_ref[:, lanes] = (out / total).astype(jnp.bfloat16)


def attend_specs():
    wide = HSTEP * DH
    return (
        pl.BlockSpec(memory_space=pltpu.SMEM),
        pl.BlockSpec((TOK, wide), lambda h: (0, h)),
        pl.BlockSpec((2, EDGE, wide), lambda h: (0, 0, h)),
        pl.BlockSpec((TOK, DH), lambda h: (0, 0)),
    )


def attend_main(pattern, query, key, value, sides):
    smem, own, side, stat = attend_specs()
    width = TOK + 4 * EDGE
    return pl.pallas_call(
        attend_main_kernel,
        out_shape=(
            jax.ShapeDtypeStruct((TOK, FEAT), jnp.float32),
            jax.ShapeDtypeStruct((TOK, DH), jnp.float32),
        ),
        grid=(HEADS // HSTEP,),
        in_specs=[smem, pl.BlockSpec((8, width), lambda h: (0, 0)), own, own, own] + [side] * 4,
        out_specs=(own, stat),
        scratch_shapes=[pltpu.VMEM((TOK, width), jnp.float32)],
        cost_estimate=pl.CostEstimate(
            flops=4 * HEADS * TOK * width * DH,
            bytes_accessed=2 * FEAT * (3 * TOK + 2 * width),
            transcendentals=HEADS * TOK * width,
        ),
        name="attend_main",
    )(pattern, jnp.asarray(key_block_ids()[:, :width]), query, key, value, *sides)


def attend_rest(pattern, query, acc, stat_in, corners):
    smem, own, side, stat = attend_specs()
    width = 2 * EDGE
    return pl.pallas_call(
        attend_rest_kernel,
        out_shape=jax.ShapeDtypeStruct((TOK, FEAT), jnp.bfloat16),
        grid=(HEADS // HSTEP,),
        in_specs=[smem, pl.BlockSpec((8, width), lambda h: (0, 0)), own, own, stat] + [side] * 2,
        out_specs=own,
        scratch_shapes=[pltpu.VMEM((TOK, width), jnp.float32)],
        cost_estimate=pl.CostEstimate(
            flops=4 * HEADS * TOK * width * DH,
            bytes_accessed=2 * FEAT * (4 * TOK + 2 * width),
            transcendentals=HEADS * TOK * width,
        ),
        name="attend_rest",
    )(pattern, jnp.asarray(key_block_ids()[:, -width:]), query, acc, stat_in, *corners)


def shift(x, axis, step):
    count = lax.axis_size(axis)
    if step > 0:
        pairs = [(i, i + 1) for i in range(count - 1)]
    else:
        pairs = [(i + 1, i) for i in range(count - 1)]
    return lax.ppermute(x, axis, pairs)


def sides_of(low, high, right, left):
    return (
        shift(low, "py", 1), shift(high, "py", -1), shift(right, "px", 1), shift(left, "px", -1)
    )


def corners_of(left, right):
    low, high = corner_parts(left, right)
    return shift(low, "py", 1), shift(high, "py", -1)


def exchange(x, axis):
    return lax.all_to_all(x, axis, 0, 0)


def everyone(x, axis, count):
    return exchange(jnp.broadcast_to(x[None], (count,) + x.shape), axis)


def per_device(queries, keys, values, pattern, targets, router_q, router_k):
    tiles_y, tiles_x = lax.axis_size("py"), lax.axis_size("px")
    tiles = tiles_y * tiles_x
    normal = float(TOPK * HEADS * 4 * tiles)
    query, key, value = (x[0].reshape(TOK, FEAT) for x in (queries, keys, values))
    aims = targets[0].transpose(0, 3, 1, 2)
    sent = pool(pattern[0], aims, query, key)
    recv = exchange(sent, TILES)
    sides = sides_of(*rims_of(keys[0], values[0]))
    me = lax.axis_index("py") * tiles_x + lax.axis_index("px")
    head = jnp.minimum(me, HEADS - 1).astype(jnp.int32).reshape(1)
    grads = router_grads(
        head, recv, router_q.swapaxes(1, 2), router_k.swapaxes(1, 2), normal
    )
    near = lax.axis_size("x") * lax.axis_size("core")
    rows = 2 * RW // near
    parts = exchange(grads.reshape(near, rows, DH), NEAR)
    part = jnp.sum(parts, axis=0)
    far = everyone(part, "far", lax.axis_size("far"))
    part = jnp.sum(far, axis=0).astype(jnp.bfloat16)
    heads = everyone(part, TILES, tiles)
    every = everyone(heads, NEAR, near)[:, :HEADS].astype(jnp.float32)
    every = every.transpose(1, 0, 2, 3).reshape(HEADS, 2 * RW, DH)
    grad_q, grad_k = (x.swapaxes(1, 2) for x in (every[:, :RW], every[:, RW:]))
    corners = corners_of(*sides[2:])
    pat = pattern.reshape(4, NOFF)
    acc, stat = attend_main(pat, query, key, value, sides)
    attended = attend_rest(pat, query, acc, stat, corners)
    return (attended.reshape(1, TILE, TILE, FEAT), grad_q, grad_k)


def solution(mesh):
    sizes = IMG_SIZES if mesh.shape["img"] == math.prod(IMG_SIZES) else (1, 1, mesh.shape["img"])
    split = Mesh(mesh.devices.reshape(sizes + mesh.devices.shape[1:]), IMG + TILES)
    return jax.shard_map(
        per_device,
        mesh=split,
        in_specs=(
            P(IMG, "py", "px", None),
            P(IMG, "py", "px", None),
            P(IMG, "py", "px", None),
            P(IMG, "py", "px", None),
            P(IMG, "py", "px", None, None),
            P(),
            P(),
        ),
        out_specs=(P(IMG, "py", "px", None), P(), P()),
        check_vma=False,
    )
```
